32 devices in a mesh: stretch: 8 (over y, x, core), fsdp: 4 (over z).
Axes of the slice: x: 2, y: 2, z: 4, core: 2. Of those that a mesh axis runs over, the one named last changes fastest.
Arguments:
- latents: bfloat16 [8, 3, 192, 6144], P('stretch', None, 'fsdp'), may hold values from -6 to 6
- step_index: int32 [8, 3], P('stretch'), may hold values from 0 to 49
- block_mask: int32 [8, 8], replicated, may hold values from 0 to 1, as said below
- mod_table: bfloat16 [50, 2, 6144], replicated, may hold values from -2 to 2
- w_query: bfloat16 [6144, 4096], P(None, 'fsdp')
- w_key: bfloat16 [6144, 4096], P(None, 'fsdp')
- w_value: bfloat16 [6144, 4096], P(None, 'fsdp'), may hold values from -0.078125 to 0.078125
Outputs:
- attended: bfloat16 [8, 3, 192, 4096], P('stretch', None, None, 'fsdp')
The draws below stay inside these ranges and needn't reach their ends.
Inputs may be any that keep to these rules, and one draw needn't show every extreme that they name: block_mask[c, c] and block_mask[c, 0] are 1 and block_mask[c, c2] is 0 for c2 > c; other entries below the diagonal are 0 or 1.
All inputs are finite; a program needn't handle non-finite values.
Results may differ from the reference program's by a relative error of at most 0.011.
Values may be sent and summed in bfloat16 or wider, within the bound.
No kernel may reach another device: no remote copies, remote signals or barrier semaphores. Data moves between devices by JAX's collectives and lax.ppermute only.
A program may use at most 192 MiB of HBM per device.

```python
import jax
import jax.numpy as jnp
from jax import lax

D = 6144
HEADS = 32
HEAD_DIM = 128
TOK = 192
STEPS = 50
VIDEOS = 3
GROUPS = 8


def common_query(key):
    return jax.random.normal(jax.random.fold_in(key, 11), (D, HEADS * HEAD_DIM), jnp.float32) * (2.0 / D) ** 0.5


def draw_w_query(key, part):
    return common_query(key).astype(jnp.bfloat16)


def draw_w_key(key, part):
    independent = jax.random.normal(jax.random.fold_in(key, 23), (D, HEADS * HEAD_DIM), jnp.float32) * (2.0 / D) ** 0.5
    mixed = independent
    return mixed.astype(jnp.bfloat16)


def draw_mod_table(key, part):
    second = jax.random.fold_in(key, 37)
    third = jax.random.fold_in(key, 41)
    scale = jax.random.uniform(second, (STEPS, D), jnp.float32, -0.5, 0.5)
    shift = jax.random.uniform(third, (STEPS, D), jnp.float32, -0.5, 0.5)
    scale = jnp.clip(scale, -2.0, 2.0)
    shift = jnp.clip(shift, -2.0, 2.0)
    return jnp.stack([scale, shift], axis=1).astype(jnp.bfloat16)


def draw_block_mask(key, part):
    draws = jax.random.randint(jax.random.fold_in(key, 5), (GROUPS, GROUPS), 0, 4)
    rows = jnp.arange(GROUPS, dtype=jnp.int32)[:, None]
    cols = jnp.arange(GROUPS, dtype=jnp.int32)[None, :]
    below = (draws > 0) & (rows > cols)
    keep = below | (rows == cols) | (cols == 0)
    return jnp.where(keep, 1, 0).astype(jnp.int32)


def touch_ends(values, own_key, low, largest):
    extent = values.shape
    spot = [jax.random.randint(jax.random.fold_in(own_key, axis), (), 0, extent[axis]) for axis in range(len(extent))]
    values = values.at[tuple(spot)].set(low)
    longest = extent.index(max(extent))
    spot[longest] = (spot[longest] + 1) % extent[longest]
    return values.at[tuple(spot)].set(largest)


def block_scale(own_key, extent, cuts, smallest, top_value):
    level, own = 1.0, jax.random.fold_in(own_key, 6)
    for axis_at, blocks in cuts:
        steps = jnp.exp(jax.random.uniform(jax.random.fold_in(own, axis_at), (blocks,), jnp.float32, smallest / len(cuts), top_value / len(cuts)))
        level = level * jnp.repeat(steps, extent[axis_at] // blocks).reshape([-1 if axis == axis_at else 1 for axis in range(len(extent))])
    return level


def gaussian(own_key, shape, spread, most, split=(), kind=jnp.bfloat16):
    values = spread * jax.random.normal(own_key, shape, jnp.float32)
    if split:
        values = values * block_scale(own_key, shape, split, -0.22, 0.18)
    return jnp.clip(values, -most, most).astype(kind)


def setup_inputs(seed: int = 0) -> dict:
    key_of = jax.random.split(jax.random.key(seed), 8)
    latents = gaussian(key_of[0], (GROUPS, VIDEOS, TOK, D), 1.0, 6.0, ((0, 8), (2, 4)))
    step_index = touch_ends(jax.random.randint(key_of[1], (GROUPS, VIDEOS), 0, STEPS), jax.random.fold_in(key_of[1], 1), 0, STEPS - 1).astype(jnp.int32)
    block_mask = draw_block_mask(jax.random.fold_in(key_of[7], 71), 0)
    mod_table = draw_mod_table(jax.random.fold_in(key_of[7], 71), 0)
    w_query = draw_w_query(jax.random.fold_in(key_of[7], 71), 0)
    w_key = draw_w_key(jax.random.fold_in(key_of[7], 71), 0)
    w_value = gaussian(key_of[6], (D, HEADS * HEAD_DIM), D ** -0.5, 0.078125, ((1, 4),))
    return {"latents": latents, "step_index": step_index, "block_mask": block_mask, "mod_table": mod_table, "w_query": w_query, "w_key": w_key, "w_value": w_value}


def modulate(latents, step_index, mod_table):
    values = latents.astype(jnp.float32)
    normed = values * lax.rsqrt(lax.optimization_barrier(jnp.mean(values * values, axis=-1, keepdims=True)) + 1e-06)
    onehot = (step_index[..., None] == jnp.arange(STEPS, dtype=jnp.int32)).astype(jnp.float32)
    mods = jnp.einsum('cbs,sd->cbd', onehot, mod_table.reshape(STEPS, 2 * D).astype(jnp.float32))
    scale = mods[..., :D][:, :, None, :]
    shift = mods[..., D:][:, :, None, :]
    return (normed * (1.0 + scale) + shift).astype(jnp.bfloat16)

def reference(latents, step_index, block_mask, mod_table, w_query, w_key, w_value):
    modulated = modulate(latents, step_index, mod_table).reshape(-1, D)
    shape = (GROUPS, VIDEOS, TOK, HEADS, HEAD_DIM)
    queries = jnp.dot(modulated, w_query, preferred_element_type=jnp.float32).astype(jnp.bfloat16).reshape(shape)
    keys = jnp.dot(modulated, w_key, preferred_element_type=jnp.float32).astype(jnp.bfloat16).reshape(shape)
    values = jnp.dot(modulated, w_value, preferred_element_type=jnp.float32).astype(jnp.bfloat16).reshape(shape)
    keys_wide = keys.astype(jnp.float32)
    values_wide = values.astype(jnp.float32)
    inverse = 1.0 / jnp.sqrt(jnp.float32(HEAD_DIM))

    def one_segment(index):
        query = queries[index].astype(jnp.float32)
        allowed = (block_mask[index] == 1)[None, None, None, :, None]
        scores = jnp.einsum('bqhd,nbkhd->bhqnk', query, keys_wide) * inverse
        masked = jnp.where(allowed, scores, jnp.float32(-1e+30))
        row_max = lax.optimization_barrier(jnp.max(masked, axis=(3, 4), keepdims=True))
        weights = jnp.where(allowed, jnp.exp(masked - row_max), jnp.float32(0.0))
        total = lax.optimization_barrier(jnp.sum(weights, axis=(3, 4)))
        rounded = weights.astype(jnp.bfloat16).astype(jnp.float32)
        summed = jnp.einsum('bhqnk,nbkhd->bhqd', rounded, values_wide)
        result = summed / total[..., None]
        return jnp.transpose(result, (0, 2, 1, 3)).reshape(VIDEOS, TOK, HEADS * HEAD_DIM).astype(jnp.bfloat16)
    return lax.map(one_segment, jnp.arange(GROUPS, dtype=jnp.int32))
```

```python
import functools

import jax
import jax.numpy as jnp
from jax import lax
from jax.experimental import pallas as pl
from jax.experimental.pallas import tpu as pltpu
from jax.sharding import PartitionSpec as P


HEAD_DIM = 128
LOG2E = 1.4426950408889634


def modulate(latents, step_index, mod_table):
    width = latents.shape[-1]
    levels = mod_table.shape[0]
    values = latents.astype(jnp.float32)
    normed = values * lax.rsqrt(jnp.mean(values * values, axis=-1, keepdims=True) + 1e-06)
    onehot = (step_index[..., None] == jnp.arange(levels, dtype=jnp.int32)).astype(jnp.bfloat16)
    mods = jnp.einsum(
        "cbs,sd->cbd",
        onehot,
        mod_table.reshape(levels, 2 * width),
        preferred_element_type=jnp.float32,
    )
    scale = mods[..., :width][:, :, None, :]
    shift = mods[..., width:][:, :, None, :]
    return (normed * (1.0 + scale) + shift).astype(jnp.bfloat16)


def plain_shards(latents, step_index, block_mask, mod_table, w_query, w_key, w_value):
    modulated = modulate(latents, step_index, mod_table)
    width = modulated.shape[-1]
    local_cols = w_query.shape[1]
    w_joined = jnp.concatenate([w_query, w_key, w_value], axis=1)
    piece = lax.all_gather(modulated, "fsdp", axis=2, tiled=True)
    flat = piece.reshape(-1, width)
    result = jnp.dot(flat, w_joined, preferred_element_type=jnp.float32).astype(jnp.bfloat16)
    projected = result.reshape(piece.shape[0], piece.shape[1], piece.shape[2], 3 * local_cols)
    videos, tokens = projected.shape[1:3]
    heads = local_cols // HEAD_DIM
    queries = projected[0, ..., :local_cols].reshape(videos, tokens, heads, HEAD_DIM)
    keys = lax.all_gather(projected[..., local_cols : 2 * local_cols], "stretch", axis=0, tiled=True)
    values = lax.all_gather(projected[..., 2 * local_cols :], "stretch", axis=0, tiled=True)
    keys = keys.reshape(-1, videos, tokens, heads, HEAD_DIM)
    values = values.reshape(-1, videos, tokens, heads, HEAD_DIM)
    mask_row = lax.dynamic_slice_in_dim(block_mask, lax.axis_index("stretch"), 1, 0)[0]
    allowed = (mask_row > 0)[None, None, None, :, None]
    scores = jnp.einsum("bqhd,nbkhd->bhqnk", queries, keys, preferred_element_type=jnp.float32)
    scores = scores * (1.0 / jnp.sqrt(jnp.float32(HEAD_DIM)))
    masked = jnp.where(allowed, scores, jnp.float32(-1e30))
    row_max = jnp.max(masked, axis=(3, 4), keepdims=True)
    weights = jnp.where(allowed, jnp.exp(masked - row_max), jnp.float32(0.0))
    total = jnp.sum(weights, axis=(3, 4))
    summed = jnp.einsum(
        "bhqnk,nbkhd->bhqd", weights.astype(jnp.bfloat16), values, preferred_element_type=jnp.float32
    )
    result = jnp.transpose(summed / total[..., None], (0, 2, 1, 3))
    return result.reshape(1, videos, tokens, local_cols).astype(jnp.bfloat16)


def hold_kernel(*refs):
    *refs, sems = refs
    count = len(refs) // 2
    copies = []
    for index, (source, target) in enumerate(zip(refs[:count], refs[count:])):
        for group in range(target.shape[0]):
            columns = slice(group * target.shape[2], (group + 1) * target.shape[2])
            copies.append(pltpu.make_async_copy(source.at[:, columns], target.at[group], sems.at[index, group]))
    for copy in copies:
        copy.start()
    for copy in copies:
        copy.wait()


def hold(*arrays):
    width, columns = arrays[0].shape
    wide = 2 * HEAD_DIM
    groups = columns // wide
    arrays = [pltpu.with_memory_space_constraint(array, pltpu.HBM) for array in arrays]
    return pl.pallas_call(
        hold_kernel,
        out_shape=[pltpu.VMEM((groups, width, wide), array.dtype) for array in arrays],
        in_specs=[pl.BlockSpec(memory_space=pltpu.HBM)] * len(arrays),
        out_specs=[pl.BlockSpec(memory_space=pltpu.VMEM)] * len(arrays),
        scratch_shapes=[pltpu.SemaphoreType.DMA((len(arrays), groups))],
        compiler_params=pltpu.CompilerParams(vmem_limit_bytes=1 << 20),
        cost_estimate=pl.CostEstimate(
            flops=0, bytes_accessed=len(arrays) * width * columns * 2, transcendentals=0
        ),
    )(*arrays)


def modulate_kernel(steps_ref, own_ref, below_ref, above_ref, far_ref, farthest_ref, mod_ref, x_ref):
    place = lax.axis_index("fsdp")
    ranks = 4
    share = own_ref.shape[0]
    rows = 16
    gain = 1.0 + mod_ref[0, 0:1, :].astype(jnp.float32)
    shift = mod_ref[0, 1:2, :].astype(jnp.float32)

    def fill(piece, slot):
        @pl.loop(0, share // rows)
        def _(row):
            inside = pl.multiple_of(row * rows, rows)
            values = piece[pl.ds(inside, rows), :].astype(jnp.float32)
            mean = jnp.mean(values * values, axis=-1, keepdims=True)
            normed = values * lax.rsqrt(mean + 1e-06)
            start = pl.multiple_of(slot * share + inside, rows)
            x_ref[pl.ds(start, rows), :] = (normed * gain + shift).astype(jnp.bfloat16)

    fill(own_ref, place)
    fill(far_ref, lax.rem(place + 2, ranks))
    pl.when(place >= 1)(lambda: fill(below_ref, place - 1))
    pl.when(place <= ranks - 2)(lambda: fill(above_ref, place + 1))
    pl.when((place == 0) | (place == ranks - 1))(lambda: fill(farthest_ref, ranks - 1 - place))


def modulate_pieces(video, steps, pieces, mod_table):
    share, width = pieces[0].shape
    tokens = share * 4
    whole = pl.BlockSpec(memory_space=pltpu.VMEM)
    return pl.pallas_call(
        modulate_kernel,
        out_shape=pltpu.VMEM((tokens, width), jnp.bfloat16),
        grid_spec=pltpu.PrefetchScalarGridSpec(
            num_scalar_prefetch=1,
            grid=(1,),
            in_specs=[whole] * len(pieces)
            + [pl.BlockSpec((1, 2, width), lambda j, steps: (steps[video], 0, 0), pipeline_mode=pl.Buffered(1))],
            out_specs=whole,
        ),
        compiler_params=pltpu.CompilerParams(vmem_limit_bytes=10 << 20),
        cost_estimate=pl.CostEstimate(flops=10 * tokens * width, bytes_accessed=4 * tokens * width, transcendentals=0),
    )(steps, *pieces, mod_table)


def project_kernel(pairs, x_ref, wq_ref, wk_ref, wv_ref, *out_refs):
    own = lax.axis_index("stretch")
    odd = lax.rem(own, 2)
    for index, pair in enumerate(pairs):
        for part, w_ref in enumerate((wq_ref, wk_ref, wv_ref)):
            result = jnp.dot(x_ref[...], w_ref[own // 2 ^ pair], preferred_element_type=jnp.float32)
            result = result.astype(jnp.bfloat16)
            low, high = result[:, :HEAD_DIM], result[:, HEAD_DIM:]
            place = slice(part * HEAD_DIM, (part + 1) * HEAD_DIM)
            out_refs[2 * index][:, place] = jnp.where(odd == 0, low, high)
            out_refs[2 * index + 1][:, place] = jnp.where(odd == 0, high, low)


def project(pairs, x, weights):
    tokens, width = x.shape
    whole = pl.BlockSpec(memory_space=pltpu.VMEM)
    columns = 6 * HEAD_DIM * len(pairs)
    return pl.pallas_call(
        functools.partial(project_kernel, pairs),
        out_shape=[jax.ShapeDtypeStruct((tokens, 3 * HEAD_DIM), jnp.bfloat16)] * (2 * len(pairs)),
        in_specs=[whole] * (1 + len(weights)),
        out_specs=[whole] * (2 * len(pairs)),
        compiler_params=pltpu.CompilerParams(vmem_limit_bytes=8 << 20),
        cost_estimate=pl.CostEstimate(
            flops=2 * tokens * width * columns, bytes_accessed=2 * tokens * columns, transcendentals=0
        ),
    )(x, *weights)


def attend_kernel(mask_ref, *refs):
    groups = (len(refs) - 2) // 2
    in_refs, out_refs = refs[:groups], refs[groups : 2 * groups]
    qkv_ref, sum_ref = refs[2 * groups :]
    tokens = qkv_ref.shape[1]
    own = lax.axis_index("stretch")
    for index, ref in enumerate(in_refs):
        qkv_ref[own ^ index] = ref[...]
    factor = LOG2E / HEAD_DIM**0.5
    column = lax.broadcasted_iota(jnp.int32, (1, groups * tokens), 1) // tokens
    for seg in range(groups):
        span = (seg + 1) * tokens
        bias = jnp.zeros((1, span), jnp.float32)
        for other in range(seg + 1):
            hidden = jnp.where(mask_ref[seg, other] == 1, 0.0, -1e30).astype(jnp.float32)
            bias = jnp.where(column[:, :span] == other, hidden, bias)
        query = qkv_ref[seg, :, 0:HEAD_DIM]
        keys = qkv_ref[0 : seg + 1, :, HEAD_DIM : 2 * HEAD_DIM].reshape(span, HEAD_DIM)
        values = qkv_ref[0 : seg + 1, :, 2 * HEAD_DIM : 3 * HEAD_DIM].reshape(span, HEAD_DIM)
        scores = lax.dot_general(query, keys, (((1,), (1,)), ((), ())), preferred_element_type=jnp.float32)
        scores = scores * factor + bias
        row_max = jnp.max(scores, axis=-1, keepdims=True)
        weights = jnp.exp2(scores - row_max)
        total = jnp.sum(weights, axis=-1, keepdims=True)
        summed = jnp.dot(weights.astype(jnp.bfloat16), values, preferred_element_type=jnp.float32)
        sum_ref[seg] = (summed / total).astype(jnp.bfloat16)
    for index, ref in enumerate(out_refs):
        ref[...] = sum_ref[own ^ index]


def attend(block_mask, slots):
    groups = len(slots)
    tokens, width = slots[0].shape
    pairs = groups * (groups + 1) // 2 * tokens * tokens
    whole = pl.BlockSpec(memory_space=pltpu.VMEM)
    return pl.pallas_call(
        attend_kernel,
        out_shape=[jax.ShapeDtypeStruct((tokens, HEAD_DIM), jnp.bfloat16)] * groups,
        in_specs=[pl.BlockSpec(memory_space=pltpu.SMEM)] + [whole] * groups,
        out_specs=[whole] * groups,
        scratch_shapes=[
            pltpu.VMEM((groups, tokens, width), jnp.bfloat16),
            pltpu.VMEM((groups, tokens, HEAD_DIM), jnp.bfloat16),
        ],
        compiler_params=pltpu.CompilerParams(vmem_limit_bytes=14 << 20),
        cost_estimate=pl.CostEstimate(
            flops=4 * pairs * HEAD_DIM, bytes_accessed=4 * groups * tokens * HEAD_DIM * 2, transcendentals=pairs
        ),
    )(block_mask, *slots)


def finish_kernel(*refs):
    groups = len(refs) - 1
    out_ref = refs[-1]
    own = lax.axis_index("stretch")
    for index, ref in enumerate(refs[:groups]):
        start = pl.multiple_of((own ^ index) * HEAD_DIM, HEAD_DIM)
        out_ref[0, 0, :, pl.ds(start, HEAD_DIM)] = ref[...]


def finish(video, videos, slots, joined):
    tokens = slots[0].shape[0]
    groups = len(slots)
    whole = pl.BlockSpec(memory_space=pltpu.VMEM)
    shape = (1, 1, tokens, groups * HEAD_DIM)
    extra = () if joined is None else (joined,)

    def body(*refs):
        finish_kernel(*refs[:groups], refs[-1])

    return pl.pallas_call(
        body,
        out_shape=jax.ShapeDtypeStruct((1, videos) + shape[2:], jnp.bfloat16),
        grid=(1,),
        in_specs=[whole] * groups + [pl.BlockSpec(memory_space=pl.ANY)] * len(extra),
        out_specs=pl.BlockSpec(shape, lambda j: (0, video, 0, 0)),
        input_output_aliases={groups: 0} if extra else {},
        compiler_params=pltpu.CompilerParams(vmem_limit_bytes=4 << 20),
    )(*slots, *extra)


SENDS = (6, 7, 2, 3, 4, 5, 1)


def exchange(slots):
    n = len(slots)
    moved = dict(enumerate(slots))
    for index in SENDS:
        moved[index] = lax.ppermute(slots[index], "stretch", [(i, i ^ index) for i in range(n)])
    return [moved[index] for index in range(n)]


def shards(latents, step_index, block_mask, mod_table, w_query, w_key, w_value):
    _, videos, _, _ = latents.shape
    near_up = [(i, i + 1) for i in range(3)]
    near_down = [(i + 1, i) for i in range(3)]
    across = [(0, 2), (1, 3), (2, 0), (3, 1)]
    onward = [(2, 3), (1, 0)]
    steps = step_index[0]
    weights = hold(w_query, w_key, w_value)
    moved = []
    for video in range(videos):
        own = latents[0, video]
        far = lax.ppermute(own, "fsdp", across)
        up = lax.ppermute(own, "fsdp", near_up)
        down = lax.ppermute(own, "fsdp", near_down)
        farthest = lax.ppermute(far, "fsdp", onward)
        moved.append((own, up, down, far, farthest))
    joined = None
    for video, pieces in enumerate(moved):
        x = modulate_pieces(video, steps, pieces, mod_table)
        slots = {}
        order = ((3,), (1, 2), (0,)) if video == videos - 1 else ((3, 1, 2, 0),)
        for part in order:
            made = project(part, x, weights)
            for index, pair in enumerate(part):
                slots[2 * pair], slots[2 * pair + 1] = made[2 * index : 2 * index + 2]
        slots = exchange([slots[index] for index in range(len(slots))])
        slots = attend(block_mask, slots)
        slots = exchange(slots)
        joined = finish(video, videos, slots, joined)
    return joined


def solution(mesh):
    placed = (
        P("stretch", None, "fsdp", None),
        P("stretch", None),
        P(),
        P(),
        P(None, "fsdp"),
        P(None, "fsdp"),
        P(None, "fsdp"),
    )

    def mapped(body):
        return jax.shard_map(
            body, mesh=mesh, in_specs=placed, out_specs=P("stretch", None, None, "fsdp"), check_vma=False
        )

    def run(*args):
        latents, w_query = args[0], args[4]
        parts = mesh.shape["stretch"], mesh.shape["fsdp"]
        share = latents.shape[2] // parts[1]
        heads = w_query.shape[1] // parts[1] // HEAD_DIM
        if parts[1] == 4 and heads == parts[0] == 8 and share % 16 == 0:
            return mapped(shards)(*args)
        return mapped(plain_shards)(*args)

    return run
```

```python
import functools

import jax
import jax.numpy as jnp
from jax import lax
from jax.experimental import pallas as pl
from jax.experimental.pallas import tpu as pltpu
from jax.sharding import PartitionSpec as P


HEAD_DIM = 128
LOG2E = 1.4426950408889634


def modulate(latents, step_index, mod_table):
    width = latents.shape[-1]
    levels = mod_table.shape[0]
    values = latents.astype(jnp.float32)
    normed = values * lax.rsqrt(jnp.mean(values * values, axis=-1, keepdims=True) + 1e-06)
    onehot = (step_index[..., None] == jnp.arange(levels, dtype=jnp.int32)).astype(jnp.bfloat16)
    mods = jnp.einsum(
        "cbs,sd->cbd",
        onehot,
        mod_table.reshape(levels, 2 * width),
        preferred_element_type=jnp.float32,
    )
    scale = mods[..., :width][:, :, None, :]
    shift = mods[..., width:][:, :, None, :]
    return (normed * (1.0 + scale) + shift).astype(jnp.bfloat16)


def plain_shards(latents, step_index, block_mask, mod_table, w_query, w_key, w_value):
    modulated = modulate(latents, step_index, mod_table)
    width = modulated.shape[-1]
    local_cols = w_query.shape[1]
    w_joined = jnp.concatenate([w_query, w_key, w_value], axis=1)
    piece = lax.all_gather(modulated, "fsdp", axis=2, tiled=True)
    flat = piece.reshape(-1, width)
    result = jnp.dot(flat, w_joined, preferred_element_type=jnp.float32).astype(jnp.bfloat16)
    projected = result.reshape(piece.shape[0], piece.shape[1], piece.shape[2], 3 * local_cols)
    videos, tokens = projected.shape[1:3]
    heads = local_cols // HEAD_DIM
    queries = projected[0, ..., :local_cols].reshape(videos, tokens, heads, HEAD_DIM)
    keys = lax.all_gather(projected[..., local_cols : 2 * local_cols], "stretch", axis=0, tiled=True)
    values = lax.all_gather(projected[..., 2 * local_cols :], "stretch", axis=0, tiled=True)
    keys = keys.reshape(-1, videos, tokens, heads, HEAD_DIM)
    values = values.reshape(-1, videos, tokens, heads, HEAD_DIM)
    mask_row = lax.dynamic_slice_in_dim(block_mask, lax.axis_index("stretch"), 1, 0)[0]
    allowed = (mask_row > 0)[None, None, None, :, None]
    scores = jnp.einsum("bqhd,nbkhd->bhqnk", queries, keys, preferred_element_type=jnp.float32)
    scores = scores * (1.0 / jnp.sqrt(jnp.float32(HEAD_DIM)))
    masked = jnp.where(allowed, scores, jnp.float32(-1e30))
    row_max = jnp.max(masked, axis=(3, 4), keepdims=True)
    weights = jnp.where(allowed, jnp.exp(masked - row_max), jnp.float32(0.0))
    total = jnp.sum(weights, axis=(3, 4))
    summed = jnp.einsum(
        "bhqnk,nbkhd->bhqd", weights.astype(jnp.bfloat16), values, preferred_element_type=jnp.float32
    )
    result = jnp.transpose(summed / total[..., None], (0, 2, 1, 3))
    return result.reshape(1, videos, tokens, local_cols).astype(jnp.bfloat16)


def hold_kernel(count, *refs):
    *refs, sems = refs
    parts = (len(refs) - count) // count
    copies = []
    for index, target in enumerate(refs[count:]):
        groups, depth, wide = target.shape
        top = index % parts * depth
        for group in range(groups):
            source = refs[index // parts].at[top : top + depth, group * wide : (group + 1) * wide]
            copies.append(pltpu.make_async_copy(source, target.at[group], sems.at[index, group]))
    for copy in copies:
        copy.start()
    for copy in copies:
        copy.wait()


def hold(parts, *arrays):
    width, columns = arrays[0].shape
    wide = 2 * HEAD_DIM
    groups = columns // wide
    total = len(arrays) * parts
    arrays = [pltpu.with_memory_space_constraint(array, pltpu.HBM) for array in arrays]
    return pl.pallas_call(
        functools.partial(hold_kernel, len(arrays)),
        out_shape=[pltpu.VMEM((groups, width // parts, wide), arrays[0].dtype)] * total,
        in_specs=[pl.BlockSpec(memory_space=pltpu.HBM)] * len(arrays),
        out_specs=[pl.BlockSpec(memory_space=pltpu.VMEM)] * total,
        scratch_shapes=[pltpu.SemaphoreType.DMA((total, groups))],
        compiler_params=pltpu.CompilerParams(vmem_limit_bytes=1 << 20),
        cost_estimate=pl.CostEstimate(
            flops=0, bytes_accessed=len(arrays) * width * columns * 2, transcendentals=0
        ),
    )(*arrays)


def fill(mod_ref, x_ref, piece, slot):
    share = piece.shape[0]
    rows = 16
    gain = 1.0 + mod_ref[0, 0:1, :].astype(jnp.float32)
    shift = mod_ref[0, 1:2, :].astype(jnp.float32)

    @pl.loop(0, share // rows)
    def _(row):
        inside = pl.multiple_of(row * rows, rows)
        values = piece[pl.ds(inside, rows), :].astype(jnp.float32)
        mean = jnp.mean(values * values, axis=-1, keepdims=True)
        normed = values * lax.rsqrt(mean + 1e-06)
        start = pl.multiple_of(slot * share + inside, rows)
        x_ref[pl.ds(start, rows), :] = (normed * gain + shift).astype(jnp.bfloat16)


def early_kernel(steps_ref, own_ref, near_ref, far_ref, mod_ref, *refs):
    x_ref = refs[-1]
    place = lax.axis_index("fsdp")
    for index, piece in enumerate((own_ref, near_ref, far_ref)):
        fill(mod_ref, x_ref, piece, place ^ index)


def late_kernel(steps_ref, inner_ref, last_ref, mod_ref, *refs):
    x_ref = refs[-1]
    place = lax.axis_index("fsdp")
    inside = (place == 1) | (place == 2)
    pl.when(inside)(lambda: fill(mod_ref, x_ref, inner_ref, place ^ 3))
    pl.when(jnp.logical_not(inside))(lambda: fill(mod_ref, x_ref, last_ref, place ^ 3))


def modulate_pieces(kernel, video, steps, pieces, mod_table, extra, filled):
    share, width = pieces[0].shape
    tokens = share * 4
    whole = pl.BlockSpec(memory_space=pltpu.VMEM)
    return pl.pallas_call(
        kernel,
        out_shape=pltpu.VMEM((tokens, width), jnp.bfloat16),
        grid_spec=pltpu.PrefetchScalarGridSpec(
            num_scalar_prefetch=1,
            grid=(1,),
            in_specs=[whole] * len(pieces)
            + [pl.BlockSpec((1, 2, width), lambda j, steps: (steps[video], 0, 0), pipeline_mode=pl.Buffered(1))]
            + [whole] * len(extra),
            out_specs=whole,
        ),
        input_output_aliases={len(pieces) + 2: 0} if filled else {},
        compiler_params=pltpu.CompilerParams(vmem_limit_bytes=6 << 20),
        cost_estimate=pl.CostEstimate(
            flops=10 * share * width * len(pieces), bytes_accessed=4 * share * width * len(pieces), transcendentals=0
        ),
    )(steps, *pieces, mod_table, *extra)


def project_kernel(pairs, x_ref, *refs):
    w_refs, out_refs = refs[: -2 * len(pairs)], refs[-2 * len(pairs) :]
    parts = len(w_refs) // 3
    depth = w_refs[0].shape[1]
    own = lax.axis_index("stretch")
    odd = lax.rem(own, 2)
    for index, pair in enumerate(pairs):
        for part in range(3):
            result = sum(
                jnp.dot(
                    x_ref[:, step * depth : (step + 1) * depth],
                    w_refs[part * parts + step][own // 2 ^ pair],
                    preferred_element_type=jnp.float32,
                )
                for step in range(parts)
            ).astype(jnp.bfloat16)
            low, high = result[:, :HEAD_DIM], result[:, HEAD_DIM:]
            place = slice(part * HEAD_DIM, (part + 1) * HEAD_DIM)
            out_refs[2 * index][:, place] = jnp.where(odd == 0, low, high)
            out_refs[2 * index + 1][:, place] = jnp.where(odd == 0, high, low)


def project(pairs, x, weights):
    tokens, width = x.shape
    whole = pl.BlockSpec(memory_space=pltpu.VMEM)
    columns = 6 * HEAD_DIM * len(pairs)
    return pl.pallas_call(
        functools.partial(project_kernel, pairs),
        out_shape=[jax.ShapeDtypeStruct((tokens, 3 * HEAD_DIM), jnp.bfloat16)] * (2 * len(pairs)),
        in_specs=[whole] * (1 + len(weights)),
        out_specs=[whole] * (2 * len(pairs)),
        compiler_params=pltpu.CompilerParams(vmem_limit_bytes=5 << 20),
        cost_estimate=pl.CostEstimate(
            flops=2 * tokens * width * columns, bytes_accessed=2 * tokens * columns, transcendentals=0
        ),
    )(x, *weights)


def attend_kernel(held, mask_ref, *refs):
    *refs, qkv_ref, sum_ref = refs[held:]
    groups, tokens, _ = qkv_ref.shape
    in_refs, out_refs = refs[:groups], refs[groups:]
    own = lax.axis_index("stretch")
    for index, ref in enumerate(in_refs):
        qkv_ref[own ^ index] = ref[...]
    factor = LOG2E / HEAD_DIM**0.5
    column = lax.broadcasted_iota(jnp.int32, (1, groups * tokens), 1) // tokens
    for seg in range(groups):
        span = (seg + 1) * tokens
        bias = jnp.zeros((1, span), jnp.float32)
        for other in range(seg + 1):
            hidden = jnp.where(mask_ref[seg, other] == 1, 0.0, -1e30).astype(jnp.float32)
            bias = jnp.where(column[:, :span] == other, hidden, bias)
        query = qkv_ref[seg, :, 0:HEAD_DIM]
        keys = qkv_ref[0 : seg + 1, :, HEAD_DIM : 2 * HEAD_DIM].reshape(span, HEAD_DIM)
        values = qkv_ref[0 : seg + 1, :, 2 * HEAD_DIM : 3 * HEAD_DIM].reshape(span, HEAD_DIM)
        scores = lax.dot_general(query, keys, (((1,), (1,)), ((), ())), preferred_element_type=jnp.float32)
        scores = scores * factor + bias
        row_max = jnp.max(scores, axis=-1, keepdims=True)
        weights = jnp.exp2(scores - row_max)
        total = jnp.sum(weights, axis=-1, keepdims=True)
        summed = jnp.dot(weights.astype(jnp.bfloat16), values, preferred_element_type=jnp.float32)
        sum_ref[seg] = (summed / total).astype(jnp.bfloat16)
    for index, ref in enumerate(out_refs):
        ref[...] = sum_ref[own ^ index]


def attend(block_mask, weights, slots):
    groups = len(slots)
    tokens, width = slots[0].shape
    pairs = groups * (groups + 1) // 2 * tokens * tokens
    whole = pl.BlockSpec(memory_space=pltpu.VMEM)
    return pl.pallas_call(
        functools.partial(attend_kernel, len(weights)),
        out_shape=[jax.ShapeDtypeStruct((tokens, HEAD_DIM), jnp.bfloat16)] * groups,
        in_specs=[pl.BlockSpec(memory_space=pltpu.SMEM)] + [whole] * (len(weights) + groups),
        out_specs=[whole] * groups,
        scratch_shapes=[
            pltpu.VMEM((groups, tokens, width), jnp.bfloat16),
            pltpu.VMEM((groups, tokens, HEAD_DIM), jnp.bfloat16),
        ],
        compiler_params=pltpu.CompilerParams(vmem_limit_bytes=8 << 20),
        cost_estimate=pl.CostEstimate(
            flops=4 * pairs * HEAD_DIM, bytes_accessed=4 * groups * tokens * HEAD_DIM * 2, transcendentals=pairs
        ),
    )(block_mask, *weights, *slots)


def finish(video, videos, slots, joined):
    tokens = slots[0].shape[0]
    groups = len(slots)
    whole = pl.BlockSpec(memory_space=pltpu.VMEM)
    extra = () if joined is None else (joined,)

    def kernel(*refs):
        own = lax.axis_index("stretch")
        for index, ref in enumerate(refs[:groups]):
            column = pl.multiple_of((own ^ index) * HEAD_DIM, HEAD_DIM)
            refs[-1][0, 0, :, pl.ds(column, HEAD_DIM)] = ref[...]

    return pl.pallas_call(
        kernel,
        out_shape=jax.ShapeDtypeStruct((1, videos, tokens, groups * HEAD_DIM), jnp.bfloat16),
        grid=(1,),
        in_specs=[whole] * groups + [pl.BlockSpec(memory_space=pl.ANY)] * len(extra),
        out_specs=pl.BlockSpec((1, 1, tokens, groups * HEAD_DIM), lambda j: (0, video, 0, 0)),
        input_output_aliases={groups: 0} if extra else {},
        compiler_params=pltpu.CompilerParams(vmem_limit_bytes=4 << 20),
    )(*slots, *extra)


SENDS = (6, 7, 2, 3, 4, 5, 1)


def exchange(slots):
    n = len(slots)
    moved = dict(enumerate(slots))
    for index in SENDS:
        moved[index] = lax.ppermute(slots[index], "stretch", [(i, i ^ index) for i in range(n)])
    return [moved[index] for index in range(n)]


def shards(latents, step_index, block_mask, mod_table, w_query, w_key, w_value):
    _, videos, _, _ = latents.shape
    steps = step_index[0]
    weights = hold(4, w_query, w_key, w_value)
    moved = []
    for video in range(videos):
        own = latents[0, video]
        if not video:
            own, latents = lax.optimization_barrier((own, latents))
        far = lax.ppermute(own, "fsdp", [(i, i ^ 2) for i in range(4)])
        near = lax.ppermute(own, "fsdp", [(i, i ^ 1) for i in range(4)])
        inner = lax.ppermute(own, "fsdp", [(1, 2), (2, 1)])
        last = lax.ppermute(far, "fsdp", [(1, 0), (2, 3)])
        moved.append(((own, near, far), (inner, last)))
    joined = None
    for video, (first, second) in enumerate(moved):
        x = modulate_pieces(early_kernel, video, steps, first, mod_table, weights, False)
        x = modulate_pieces(late_kernel, video, steps, second, mod_table, (x, *weights), True)
        slots = {}
        order = ((3,), (1, 2), (0,)) if video == videos - 1 else ((3, 1, 2, 0),)
        for part in order:
            made = project(part, x, weights)
            for index, pair in enumerate(part):
                slots[2 * pair], slots[2 * pair + 1] = made[2 * index : 2 * index + 2]
        slots = exchange([slots[index] for index in range(len(slots))])
        slots = attend(block_mask, weights if video < videos - 1 else (), slots)
        slots = exchange(slots)
        joined = finish(video, videos, slots, joined)
    return joined


def solution(mesh):
    placed = (
        P("stretch", None, "fsdp", None),
        P("stretch", None),
        P(),
        P(),
        P(None, "fsdp"),
        P(None, "fsdp"),
        P(None, "fsdp"),
    )

    def mapped(body):
        return jax.shard_map(
            body, mesh=mesh, in_specs=placed, out_specs=P("stretch", None, None, "fsdp"), check_vma=False
        )

    def run(*args):
        latents, w_query = args[0], args[4]
        parts = mesh.shape["stretch"], mesh.shape["fsdp"]
        share = latents.shape[2] // parts[1]
        heads = w_query.shape[1] // parts[1] // HEAD_DIM
        if parts[1] == 4 and heads == parts[0] == 8 and share % 16 == 0:
            return mapped(shards)(*args)
        return mapped(plain_shards)(*args)

    return run
```

```python
import functools

import jax
import jax.numpy as jnp
from jax import lax
from jax.experimental import pallas as pl
from jax.experimental.pallas import tpu as pltpu
from jax.sharding import PartitionSpec as P


HEAD_DIM = 128
LOG2E = 1.4426950408889634


def modulate(latents, step_index, mod_table):
    width = latents.shape[-1]
    levels = mod_table.shape[0]
    values = latents.astype(jnp.float32)
    normed = values * lax.rsqrt(jnp.mean(values * values, axis=-1, keepdims=True) + 1e-06)
    onehot = (step_index[..., None] == jnp.arange(levels, dtype=jnp.int32)).astype(jnp.bfloat16)
    mods = jnp.einsum(
        "cbs,sd->cbd",
        onehot,
        mod_table.reshape(levels, 2 * width),
        preferred_element_type=jnp.float32,
    )
    scale = mods[..., :width][:, :, None, :]
    shift = mods[..., width:][:, :, None, :]
    return (normed * (1.0 + scale) + shift).astype(jnp.bfloat16)


def plain_shards(latents, step_index, block_mask, mod_table, w_query, w_key, w_value):
    modulated = modulate(latents, step_index, mod_table)
    width = modulated.shape[-1]
    local_cols = w_query.shape[1]
    w_joined = jnp.concatenate([w_query, w_key, w_value], axis=1)
    piece = lax.all_gather(modulated, "fsdp", axis=2, tiled=True)
    flat = piece.reshape(-1, width)
    result = jnp.dot(flat, w_joined, preferred_element_type=jnp.float32).astype(jnp.bfloat16)
    projected = result.reshape(piece.shape[0], piece.shape[1], piece.shape[2], 3 * local_cols)
    videos, tokens = projected.shape[1:3]
    heads = local_cols // HEAD_DIM
    queries = projected[0, ..., :local_cols].reshape(videos, tokens, heads, HEAD_DIM)
    keys = lax.all_gather(projected[..., local_cols : 2 * local_cols], "stretch", axis=0, tiled=True)
    values = lax.all_gather(projected[..., 2 * local_cols :], "stretch", axis=0, tiled=True)
    keys = keys.reshape(-1, videos, tokens, heads, HEAD_DIM)
    values = values.reshape(-1, videos, tokens, heads, HEAD_DIM)
    mask_row = lax.dynamic_slice_in_dim(block_mask, lax.axis_index("stretch"), 1, 0)[0]
    allowed = (mask_row > 0)[None, None, None, :, None]
    scores = jnp.einsum("bqhd,nbkhd->bhqnk", queries, keys, preferred_element_type=jnp.float32)
    scores = scores * (1.0 / jnp.sqrt(jnp.float32(HEAD_DIM)))
    masked = jnp.where(allowed, scores, jnp.float32(-1e30))
    row_max = jnp.max(masked, axis=(3, 4), keepdims=True)
    weights = jnp.where(allowed, jnp.exp(masked - row_max), jnp.float32(0.0))
    total = jnp.sum(weights, axis=(3, 4))
    summed = jnp.einsum(
        "bhqnk,nbkhd->bhqd", weights.astype(jnp.bfloat16), values, preferred_element_type=jnp.float32
    )
    result = jnp.transpose(summed / total[..., None], (0, 2, 1, 3))
    return result.reshape(1, videos, tokens, local_cols).astype(jnp.bfloat16)


def hold_kernel(count, *refs):
    *refs, sems = refs
    parts = (len(refs) - count) // count
    copies = []
    for index, target in enumerate(refs[count:]):
        groups, depth, wide = target.shape
        top = index % parts * depth
        for group in range(groups):
            source = refs[index // parts].at[top : top + depth, group * wide : (group + 1) * wide]
            copies.append(pltpu.make_async_copy(source, target.at[group], sems.at[index, group]))
    for copy in copies:
        copy.start()
    for copy in copies:
        copy.wait()


def hold(parts, *arrays):
    width, columns = arrays[0].shape
    wide = 2 * HEAD_DIM
    groups = columns // wide
    total = len(arrays) * parts
    arrays = [pltpu.with_memory_space_constraint(array, pltpu.HBM) for array in arrays]
    return pl.pallas_call(
        functools.partial(hold_kernel, len(arrays)),
        out_shape=[pltpu.VMEM((groups, width // parts, wide), arrays[0].dtype)] * total,
        in_specs=[pl.BlockSpec(memory_space=pltpu.HBM)] * len(arrays),
        out_specs=[pl.BlockSpec(memory_space=pltpu.VMEM)] * total,
        scratch_shapes=[pltpu.SemaphoreType.DMA((total, groups))],
        compiler_params=pltpu.CompilerParams(vmem_limit_bytes=1 << 20),
        cost_estimate=pl.CostEstimate(
            flops=0, bytes_accessed=len(arrays) * width * columns * 2, transcendentals=0
        ),
    )(*arrays)


def fill(mod_ref, x_ref, piece, slot):
    share = piece.shape[0]
    rows = 16
    gain = 1.0 + mod_ref[0, 0:1, :].astype(jnp.float32)
    shift = mod_ref[0, 1:2, :].astype(jnp.float32)

    @pl.loop(0, share // rows)
    def _(row):
        inside = pl.multiple_of(row * rows, rows)
        values = piece[pl.ds(inside, rows), :].astype(jnp.float32)
        mean = jnp.mean(values * values, axis=-1, keepdims=True)
        normed = values * lax.rsqrt(mean + 1e-06)
        start = pl.multiple_of(slot * share + inside, rows)
        x_ref[pl.ds(start, rows), :] = (normed * gain + shift).astype(jnp.bfloat16)


def early_kernel(steps_ref, own_ref, near_ref, far_ref, mod_ref, *refs):
    x_ref = refs[-1]
    place = lax.axis_index("fsdp")
    for index, piece in enumerate((own_ref, near_ref, far_ref)):
        fill(mod_ref, x_ref, piece, place ^ index)


def late_kernel(steps_ref, inner_ref, last_ref, mod_ref, *refs):
    x_ref = refs[-1]
    place = lax.axis_index("fsdp")
    inside = (place == 1) | (place == 2)
    pl.when(inside)(lambda: fill(mod_ref, x_ref, inner_ref, place ^ 3))
    pl.when(jnp.logical_not(inside))(lambda: fill(mod_ref, x_ref, last_ref, place ^ 3))


def modulate_pieces(kernel, video, steps, pieces, mod_table, extra, filled):
    share, width = pieces[0].shape
    tokens = share * 4
    whole = pl.BlockSpec(memory_space=pltpu.VMEM)
    return pl.pallas_call(
        kernel,
        out_shape=pltpu.VMEM((tokens, width), jnp.bfloat16),
        grid_spec=pltpu.PrefetchScalarGridSpec(
            num_scalar_prefetch=1,
            grid=(1,),
            in_specs=[whole] * len(pieces)
            + [pl.BlockSpec((1, 2, width), lambda j, steps: (steps[video], 0, 0), pipeline_mode=pl.Buffered(1))]
            + [whole] * len(extra),
            out_specs=whole,
        ),
        input_output_aliases={len(pieces) + 2: 0} if filled else {},
        compiler_params=pltpu.CompilerParams(vmem_limit_bytes=6 << 20),
        cost_estimate=pl.CostEstimate(
            flops=10 * share * width * len(pieces), bytes_accessed=4 * share * width * len(pieces), transcendentals=0
        ),
    )(steps, *pieces, mod_table, *extra)


def project_kernel(pairs, x_ref, *refs):
    w_refs, out_refs = refs[: -2 * len(pairs)], refs[-2 * len(pairs) :]
    parts = len(w_refs) // 3
    depth = w_refs[0].shape[1]
    own = lax.axis_index("stretch")
    odd = lax.rem(own, 2)
    for index, pair in enumerate(pairs):
        for part in range(3):
            result = sum(
                jnp.dot(
                    x_ref[:, step * depth : (step + 1) * depth],
                    w_refs[part * parts + step][own // 2 ^ pair],
                    preferred_element_type=jnp.float32,
                )
                for step in range(parts)
            ).astype(jnp.bfloat16)
            low, high = result[:, :HEAD_DIM], result[:, HEAD_DIM:]
            place = slice(part * HEAD_DIM, (part + 1) * HEAD_DIM)
            out_refs[2 * index][:, place] = jnp.where(odd == 0, low, high)
            out_refs[2 * index + 1][:, place] = jnp.where(odd == 0, high, low)


def project(pairs, x, weights):
    tokens, width = x.shape
    whole = pl.BlockSpec(memory_space=pltpu.VMEM)
    columns = 6 * HEAD_DIM * len(pairs)
    return pl.pallas_call(
        functools.partial(project_kernel, pairs),
        out_shape=[jax.ShapeDtypeStruct((tokens, 3 * HEAD_DIM), jnp.bfloat16)] * (2 * len(pairs)),
        in_specs=[whole] * (1 + len(weights)),
        out_specs=[whole] * (2 * len(pairs)),
        compiler_params=pltpu.CompilerParams(vmem_limit_bytes=5 << 20),
        cost_estimate=pl.CostEstimate(
            flops=2 * tokens * width * columns, bytes_accessed=2 * tokens * columns, transcendentals=0
        ),
    )(x, *weights)


def attend_kernel(held, pace, mask_ref, *refs):
    *refs, qkv_ref, sum_ref = refs[held:]
    groups, tokens, _ = qkv_ref.shape
    in_refs, out_refs = refs[:groups], refs[groups:]
    own = lax.axis_index("stretch")
    for index, ref in enumerate(in_refs):
        qkv_ref[own ^ index] = ref[...]
    factor = LOG2E / HEAD_DIM**0.5
    column = lax.broadcasted_iota(jnp.int32, (1, groups * tokens), 1) // tokens
    for first in range(0, groups, pace):
        last = min(first + pace, groups)
        span = last * tokens

        def one(seg):
            bias = jnp.zeros((1, span), jnp.float32)
            for other in range(last):
                hidden = jnp.where(mask_ref[seg, other] == 1, 0.0, -1e30).astype(jnp.float32)
                bias = jnp.where(column[:, :span] == other, hidden, bias)
            query = qkv_ref[seg, :, 0:HEAD_DIM]
            keys = qkv_ref[0:last, :, HEAD_DIM : 2 * HEAD_DIM].reshape(span, HEAD_DIM)
            values = qkv_ref[0:last, :, 2 * HEAD_DIM : 3 * HEAD_DIM].reshape(span, HEAD_DIM)
            scores = lax.dot_general(query, keys, (((1,), (1,)), ((), ())), preferred_element_type=jnp.float32)
            scores = scores * factor + bias
            row_max = jnp.max(scores, axis=-1, keepdims=True)
            weights = jnp.exp2(scores - row_max)
            total = jnp.sum(weights, axis=-1, keepdims=True)
            summed = jnp.dot(weights.astype(jnp.bfloat16), values, preferred_element_type=jnp.float32)
            sum_ref[seg] = (summed / total).astype(jnp.bfloat16)

        if last - first == 1:
            one(first)
        else:
            pl.loop(first, last)(one)

    for index, ref in enumerate(out_refs):
        ref[...] = sum_ref[own ^ index]


def attend(pace, block_mask, weights, slots):
    groups = len(slots)
    tokens, width = slots[0].shape
    pairs = groups * (groups + 1) // 2 * tokens * tokens
    whole = pl.BlockSpec(memory_space=pltpu.VMEM)
    return pl.pallas_call(
        functools.partial(attend_kernel, len(weights), pace),
        out_shape=[jax.ShapeDtypeStruct((tokens, HEAD_DIM), jnp.bfloat16)] * groups,
        in_specs=[pl.BlockSpec(memory_space=pltpu.SMEM)] + [whole] * (len(weights) + groups),
        out_specs=[whole] * groups,
        scratch_shapes=[
            pltpu.VMEM((groups, tokens, width), jnp.bfloat16),
            pltpu.VMEM((groups, tokens, HEAD_DIM), jnp.bfloat16),
        ],
        compiler_params=pltpu.CompilerParams(vmem_limit_bytes=8 << 20),
        cost_estimate=pl.CostEstimate(
            flops=4 * pairs * HEAD_DIM, bytes_accessed=4 * groups * tokens * HEAD_DIM * 2, transcendentals=pairs
        ),
    )(block_mask, *weights, *slots)


def finish(video, videos, slots, joined):
    tokens = slots[0].shape[0]
    groups = len(slots)
    whole = pl.BlockSpec(memory_space=pltpu.VMEM)
    extra = () if joined is None else (joined,)

    def kernel(*refs):
        own = lax.axis_index("stretch")
        for index, ref in enumerate(refs[:groups]):
            column = pl.multiple_of((own ^ index) * HEAD_DIM, HEAD_DIM)
            refs[-1][0, 0, :, pl.ds(column, HEAD_DIM)] = ref[...]

    return pl.pallas_call(
        kernel,
        out_shape=jax.ShapeDtypeStruct((1, videos, tokens, groups * HEAD_DIM), jnp.bfloat16),
        grid=(1,),
        in_specs=[whole] * groups + [pl.BlockSpec(memory_space=pl.ANY)] * len(extra),
        out_specs=pl.BlockSpec((1, 1, tokens, groups * HEAD_DIM), lambda j: (0, video, 0, 0)),
        input_output_aliases={groups: 0} if extra else {},
        compiler_params=pltpu.CompilerParams(vmem_limit_bytes=4 << 20),
    )(*slots, *extra)


SENDS = (6, 7, 2, 3, 4, 5, 1)


def exchange(slots):
    n = len(slots)
    moved = dict(enumerate(slots))
    for index in SENDS:
        moved[index] = lax.ppermute(slots[index], "stretch", [(i, i ^ index) for i in range(n)])
    return [moved[index] for index in range(n)]


def shards(latents, step_index, block_mask, mod_table, w_query, w_key, w_value):
    _, videos, _, _ = latents.shape
    steps = step_index[0]
    weights = hold(4, w_query, w_key, w_value)
    moved = []
    for video in range(videos):
        own = latents[0, video]
        if not video:
            own, latents = lax.optimization_barrier((own, latents))
        far = lax.ppermute(own, "fsdp", [(i, i ^ 2) for i in range(4)])
        near = lax.ppermute(own, "fsdp", [(i, i ^ 1) for i in range(4)])
        inner = lax.ppermute(own, "fsdp", [(1, 2), (2, 1)])
        last = lax.ppermute(far, "fsdp", [(1, 0), (2, 3)])
        moved.append(((own, near, far), (inner, last)))
    joined = None
    for video, (first, second) in enumerate(moved):
        x = modulate_pieces(early_kernel, video, steps, first, mod_table, weights, False)
        x = modulate_pieces(late_kernel, video, steps, second, mod_table, (x, *weights), True)
        slots = {}
        order = ((3,), (1, 2), (0,)) if video == videos - 1 else ((3, 1, 2, 0),)
        for part in order:
            made = project(part, x, weights)
            for index, pair in enumerate(part):
                slots[2 * pair], slots[2 * pair + 1] = made[2 * index : 2 * index + 2]
        slots = exchange([slots[index] for index in range(len(slots))])
        slots = attend(1 if video else 2, block_mask, weights if video < videos - 1 else (), slots)
        slots = exchange(slots)
        joined = finish(video, videos, slots, joined)
    return joined


def solution(mesh):
    placed = (
        P("stretch", None, "fsdp", None),
        P("stretch", None),
        P(),
        P(),
        P(None, "fsdp"),
        P(None, "fsdp"),
        P(None, "fsdp"),
    )

    def mapped(body):
        return jax.shard_map(
            body, mesh=mesh, in_specs=placed, out_specs=P("stretch", None, None, "fsdp"), check_vma=False
        )

    def run(*args):
        latents, w_query = args[0], args[4]
        parts = mesh.shape["stretch"], mesh.shape["fsdp"]
        share = latents.shape[2] // parts[1]
        heads = w_query.shape[1] // parts[1] // HEAD_DIM
        if parts[1] == 4 and heads == parts[0] == 8 and share % 16 == 0:
            return mapped(shards)(*args)
        return mapped(plain_shards)(*args)

    return run
```

```python
import functools

import jax
import jax.numpy as jnp
from jax import lax
from jax.experimental import pallas as pl
from jax.experimental.pallas import tpu as pltpu
from jax.sharding import PartitionSpec as P


HEAD_DIM = 128
LOG2E = 1.4426950408889634


def modulate(latents, step_index, mod_table):
    width = latents.shape[-1]
    levels = mod_table.shape[0]
    values = latents.astype(jnp.float32)
    normed = values * lax.rsqrt(jnp.mean(values * values, axis=-1, keepdims=True) + 1e-06)
    onehot = (step_index[..., None] == jnp.arange(levels, dtype=jnp.int32)).astype(jnp.bfloat16)
    mods = jnp.einsum(
        "cbs,sd->cbd",
        onehot,
        mod_table.reshape(levels, 2 * width),
        preferred_element_type=jnp.float32,
    )
    scale = mods[..., :width][:, :, None, :]
    shift = mods[..., width:][:, :, None, :]
    return (normed * (1.0 + scale) + shift).astype(jnp.bfloat16)


def plain_shards(latents, step_index, block_mask, mod_table, w_query, w_key, w_value):
    modulated = modulate(latents, step_index, mod_table)
    width = modulated.shape[-1]
    local_cols = w_query.shape[1]
    w_joined = jnp.concatenate([w_query, w_key, w_value], axis=1)
    piece = lax.all_gather(modulated, "fsdp", axis=2, tiled=True)
    flat = piece.reshape(-1, width)
    result = jnp.dot(flat, w_joined, preferred_element_type=jnp.float32).astype(jnp.bfloat16)
    projected = result.reshape(piece.shape[0], piece.shape[1], piece.shape[2], 3 * local_cols)
    videos, tokens = projected.shape[1:3]
    heads = local_cols // HEAD_DIM
    queries = projected[0, ..., :local_cols].reshape(videos, tokens, heads, HEAD_DIM)
    keys = lax.all_gather(projected[..., local_cols : 2 * local_cols], "stretch", axis=0, tiled=True)
    values = lax.all_gather(projected[..., 2 * local_cols :], "stretch", axis=0, tiled=True)
    keys = keys.reshape(-1, videos, tokens, heads, HEAD_DIM)
    values = values.reshape(-1, videos, tokens, heads, HEAD_DIM)
    mask_row = lax.dynamic_slice_in_dim(block_mask, lax.axis_index("stretch"), 1, 0)[0]
    allowed = (mask_row > 0)[None, None, None, :, None]
    scores = jnp.einsum("bqhd,nbkhd->bhqnk", queries, keys, preferred_element_type=jnp.float32)
    scores = scores * (1.0 / jnp.sqrt(jnp.float32(HEAD_DIM)))
    masked = jnp.where(allowed, scores, jnp.float32(-1e30))
    row_max = jnp.max(masked, axis=(3, 4), keepdims=True)
    weights = jnp.where(allowed, jnp.exp(masked - row_max), jnp.float32(0.0))
    total = jnp.sum(weights, axis=(3, 4))
    summed = jnp.einsum(
        "bhqnk,nbkhd->bhqd", weights.astype(jnp.bfloat16), values, preferred_element_type=jnp.float32
    )
    result = jnp.transpose(summed / total[..., None], (0, 2, 1, 3))
    return result.reshape(1, videos, tokens, local_cols).astype(jnp.bfloat16)


def hold_kernel(count, *refs):
    *refs, sems = refs
    parts = (len(refs) - count) // count
    copies = []
    for index, target in enumerate(refs[count:]):
        groups, depth, wide = target.shape
        top = index % parts * depth
        for group in range(groups):
            source = refs[index // parts].at[top : top + depth, group * wide : (group + 1) * wide]
            copies.append(pltpu.make_async_copy(source, target.at[group], sems.at[index, group]))
    for copy in copies:
        copy.start()
    for copy in copies:
        copy.wait()


def hold(parts, *arrays):
    width, columns = arrays[0].shape
    wide = 2 * HEAD_DIM
    groups = columns // wide
    total = len(arrays) * parts
    arrays = [pltpu.with_memory_space_constraint(array, pltpu.HBM) for array in arrays]
    return pl.pallas_call(
        functools.partial(hold_kernel, len(arrays)),
        out_shape=[pltpu.VMEM((groups, width // parts, wide), arrays[0].dtype)] * total,
        in_specs=[pl.BlockSpec(memory_space=pltpu.HBM)] * len(arrays),
        out_specs=[pl.BlockSpec(memory_space=pltpu.VMEM)] * total,
        scratch_shapes=[pltpu.SemaphoreType.DMA((total, groups))],
        compiler_params=pltpu.CompilerParams(vmem_limit_bytes=1 << 20),
        cost_estimate=pl.CostEstimate(
            flops=0, bytes_accessed=len(arrays) * width * columns * 2, transcendentals=0
        ),
    )(*arrays)


PIECES = (0, 2, 1, 3)


def fill(mod_ref, x_ref, piece, index):
    share = piece.shape[0]
    rows = 16
    gain = 1.0 + mod_ref[0, 0:1, :].astype(jnp.float32)
    shift = mod_ref[0, 1:2, :].astype(jnp.float32)

    @pl.loop(0, share // rows)
    def _(row):
        inside = pl.multiple_of(row * rows, rows)
        values = piece[pl.ds(inside, rows), :].astype(jnp.float32)
        mean = jnp.mean(values * values, axis=-1, keepdims=True)
        normed = values * lax.rsqrt(mean + 1e-06)
        start = pl.multiple_of(index * share + inside, rows)
        x_ref[pl.ds(start, rows), :] = (normed * gain + shift).astype(jnp.bfloat16)


def early_kernel(first, count, steps_ref, *refs):
    for index in range(count):
        fill(refs[count], refs[-1], refs[index], first + index)


def late_kernel(steps_ref, inner_ref, last_ref, mod_ref, *refs):
    place = lax.axis_index("fsdp")
    inside = (place == 1) | (place == 2)
    pl.when(inside)(lambda: fill(mod_ref, refs[-1], inner_ref, 3))
    pl.when(jnp.logical_not(inside))(lambda: fill(mod_ref, refs[-1], last_ref, 3))


def modulate_pieces(kernel, video, steps, pieces, mod_table, extra, filled):
    share, width = pieces[0].shape
    tokens = share * 4
    whole = pl.BlockSpec(memory_space=pltpu.VMEM)
    return pl.pallas_call(
        kernel,
        out_shape=pltpu.VMEM((tokens, width), jnp.bfloat16),
        grid_spec=pltpu.PrefetchScalarGridSpec(
            num_scalar_prefetch=1,
            grid=(1,),
            in_specs=[whole] * len(pieces)
            + [pl.BlockSpec((1, 2, width), lambda j, steps: (steps[video], 0, 0), pipeline_mode=pl.Buffered(1))]
            + [whole] * len(extra),
            out_specs=whole,
        ),
        input_output_aliases={len(pieces) + 2: 0} if filled else {},
        compiler_params=pltpu.CompilerParams(vmem_limit_bytes=6 << 20),
        cost_estimate=pl.CostEstimate(
            flops=10 * share * width * len(pieces), bytes_accessed=4 * share * width * len(pieces), transcendentals=0
        ),
    )(steps, *pieces, mod_table, *extra)


def project_pair(pair, rows, x_ref, w_refs, even_ref, odd_ref):
    own = lax.axis_index("stretch")
    odd = lax.rem(own, 2)
    parts = len(w_refs) // 3
    depth = w_refs[0].shape[1]
    for part in range(3):
        result = sum(
            jnp.dot(
                x_ref[rows[0] : rows[1], step * depth : (step + 1) * depth],
                w_refs[part * parts + step][own // 2 ^ pair],
                preferred_element_type=jnp.float32,
            )
            for step in range(parts)
        ).astype(jnp.bfloat16)
        low, high = result[:, :HEAD_DIM], result[:, HEAD_DIM:]
        place = slice(part * HEAD_DIM, (part + 1) * HEAD_DIM)
        even_ref[:, place] = jnp.where(odd == 0, low, high)
        odd_ref[:, place] = jnp.where(odd == 0, high, low)


def project_kernel(pairs, rows, x_ref, *refs):
    w_refs, out_refs = refs[: -2 * len(pairs)], refs[-2 * len(pairs) :]
    for index, pair in enumerate(pairs):
        project_pair(pair, rows, x_ref, w_refs, out_refs[2 * index], out_refs[2 * index + 1])


def project_loop_kernel(pairs, rows, x_ref, *refs):
    *w_refs, made_ref = refs[: -2 * len(pairs) - 1] + refs[-1:]
    out_refs = refs[-2 * len(pairs) - 1 : -1]

    @pl.loop(0, len(pairs))
    def _(pair):
        project_pair(pair, rows, x_ref, w_refs, made_ref.at[2 * pair], made_ref.at[2 * pair + 1])

    for index, ref in enumerate(out_refs):
        ref[...] = made_ref[index]


def project(pairs, rows, x, weights, short=False):
    tokens, width = rows[1] - rows[0], x.shape[1]
    whole = pl.BlockSpec(memory_space=pltpu.VMEM)
    columns = 6 * HEAD_DIM * len(pairs)
    return pl.pallas_call(
        functools.partial(project_loop_kernel if short else project_kernel, pairs, rows),
        out_shape=[jax.ShapeDtypeStruct((tokens, 3 * HEAD_DIM), jnp.bfloat16)] * (2 * len(pairs)),
        in_specs=[whole] * (1 + len(weights)),
        out_specs=[whole] * (2 * len(pairs)),
        scratch_shapes=[pltpu.VMEM((2 * len(pairs), tokens, 3 * HEAD_DIM), jnp.bfloat16)] * short,
        compiler_params=pltpu.CompilerParams(vmem_limit_bytes=(6 if short else 5) << 20),
        cost_estimate=pl.CostEstimate(
            flops=2 * tokens * width * columns, bytes_accessed=2 * tokens * columns, transcendentals=0
        ),
    )(x, *weights)


def attend_kernel(held, pace, counts, mask_ref, *refs):
    *refs, qkv_ref, sum_ref = refs[held:]
    groups, tokens, _ = qkv_ref.shape
    in_refs, out_refs = refs[: sum(counts)], refs[sum(counts) :]
    own = lax.axis_index("stretch")
    for index, count in enumerate(counts):
        row = 0
        for ref in in_refs[sum(counts[:index]) : sum(counts[:index]) + count]:
            qkv_ref[own ^ index, row : row + ref.shape[0], :] = ref[...]
            row += ref.shape[0]
    factor = LOG2E / HEAD_DIM**0.5
    column = lax.broadcasted_iota(jnp.int32, (1, groups * tokens), 1) // tokens
    for first in range(0, groups, pace):
        last = min(first + pace, groups)
        span = last * tokens

        def one(seg):
            bias = jnp.zeros((1, span), jnp.float32)
            for other in range(last):
                hidden = jnp.where(mask_ref[seg, other] == 1, 0.0, -1e30).astype(jnp.float32)
                bias = jnp.where(column[:, :span] == other, hidden, bias)
            query = qkv_ref[seg, :, 0:HEAD_DIM]
            keys = qkv_ref[0:last, :, HEAD_DIM : 2 * HEAD_DIM].reshape(span, HEAD_DIM)
            values = qkv_ref[0:last, :, 2 * HEAD_DIM : 3 * HEAD_DIM].reshape(span, HEAD_DIM)
            scores = lax.dot_general(query, keys, (((1,), (1,)), ((), ())), preferred_element_type=jnp.float32)
            scores = scores * factor + bias
            row_max = jnp.max(scores, axis=-1, keepdims=True)
            weights = jnp.exp2(scores - row_max)
            total = jnp.sum(weights, axis=-1, keepdims=True)
            summed = jnp.dot(weights.astype(jnp.bfloat16), values, preferred_element_type=jnp.float32)
            sum_ref[seg] = (summed / total).astype(jnp.bfloat16)

        if last - first == 1:
            one(first)
        else:
            pl.loop(first, last)(one)

    for index, ref in enumerate(out_refs):
        ref[...] = sum_ref[own ^ index]


def attend(pace, block_mask, weights, slots):
    groups = len(slots)
    counts = [len(slot) for slot in slots]
    tokens, width = sum(part.shape[0] for part in slots[0]), slots[0][0].shape[1]
    pairs = groups * (groups + 1) // 2 * tokens * tokens
    whole = pl.BlockSpec(memory_space=pltpu.VMEM)
    return pl.pallas_call(
        functools.partial(attend_kernel, len(weights), pace, counts),
        out_shape=[jax.ShapeDtypeStruct((tokens, HEAD_DIM), jnp.bfloat16)] * groups,
        in_specs=[pl.BlockSpec(memory_space=pltpu.SMEM)] + [whole] * (len(weights) + sum(counts)),
        out_specs=[whole] * groups,
        scratch_shapes=[
            pltpu.VMEM((groups, tokens, width), jnp.bfloat16),
            pltpu.VMEM((groups, tokens, HEAD_DIM), jnp.bfloat16),
        ],
        compiler_params=pltpu.CompilerParams(vmem_limit_bytes=8 << 20),
        cost_estimate=pl.CostEstimate(
            flops=4 * pairs * HEAD_DIM, bytes_accessed=4 * groups * tokens * HEAD_DIM * 2, transcendentals=pairs
        ),
    )(block_mask, *weights, *[part for slot in slots for part in slot])


def finish(video, videos, slots, joined):
    tokens = slots[0].shape[0]
    groups = len(slots)
    whole = pl.BlockSpec(memory_space=pltpu.VMEM)
    extra = () if joined is None else (joined,)

    def kernel(*refs):
        own, place = lax.axis_index("stretch"), lax.axis_index("fsdp")
        share = tokens // len(PIECES)
        for index, ref in enumerate(refs[:groups]):
            column = pl.multiple_of((own ^ index) * HEAD_DIM, HEAD_DIM)
            for piece, distance in enumerate(PIECES):
                row = pl.multiple_of((place ^ distance) * share, 16)
                refs[-1][0, 0, pl.ds(row, share), pl.ds(column, HEAD_DIM)] = ref[piece * share : (piece + 1) * share, :]

    return pl.pallas_call(
        kernel,
        out_shape=jax.ShapeDtypeStruct((1, videos, tokens, groups * HEAD_DIM), jnp.bfloat16),
        grid=(1,),
        in_specs=[whole] * groups + [pl.BlockSpec(memory_space=pl.ANY)] * len(extra),
        out_specs=pl.BlockSpec((1, 1, tokens, groups * HEAD_DIM), lambda j: (0, video, 0, 0)),
        input_output_aliases={groups: 0} if extra else {},
        compiler_params=pltpu.CompilerParams(vmem_limit_bytes=4 << 20),
    )(*slots, *extra)


SENDS = (6, 7, 2, 3, 4, 5, 1)


def exchange(slots):
    n = lax.axis_size("stretch")
    moved = dict(slots)
    for index in SENDS:
        if index in slots:
            moved[index] = lax.ppermute(slots[index], "stretch", [(i, i ^ index) for i in range(n)])
    return moved


def shards(latents, step_index, block_mask, mod_table, w_query, w_key, w_value):
    _, videos, share, _ = latents.shape
    steps = step_index[0]
    weights = hold(4, w_query, w_key, w_value)
    moved = []
    for video in range(videos):
        own = latents[0, video]
        if not video:
            own, latents = lax.optimization_barrier((own, latents))
        far = lax.ppermute(own, "fsdp", [(i, i ^ 2) for i in range(4)])
        near = lax.ppermute(own, "fsdp", [(i, i ^ 1) for i in range(4)])
        inner = lax.ppermute(own, "fsdp", [(1, 2), (2, 1)])
        last = lax.ppermute(far, "fsdp", [(1, 0), (2, 3)])
        moved.append(((own, far, near), (inner, last)))
    joined = None
    tokens = share * 4
    half = 2 * share
    for video, (first, second) in enumerate(moved):
        final = video == videos - 1
        early = (first[: 1 + final], first[1 + final :]) if video else (first,)
        x, soon, place = None, {}, 0
        for pieces in early:
            kernel = functools.partial(early_kernel, place, len(pieces))
            x = modulate_pieces(kernel, video, steps, pieces, mod_table, (x, *weights)[x is None :], x is not None)
            if final and not place:
                soon = dict(zip((4, 5), project((2,), (0, half), x, weights)))
                soon = exchange(soon)
            place += len(pieces)
        x = modulate_pieces(late_kernel, video, steps, second, mod_table, (x, *weights), True)
        slots = {}
        order = ((3,), (1,), (2,), (0,)) if final else ((0, 1, 2, 3),)
        for part in order:
            rows = (half, tokens) if final and part[0] == 2 else (0, tokens)
            made = project(part, rows, x, weights, short=not video)
            for index, pair in enumerate(part):
                slots[2 * pair], slots[2 * pair + 1] = made[2 * index : 2 * index + 2]
        slots = exchange(slots)
        slots = [(soon[index], slots[index]) if index in soon else (slots[index],) for index in range(len(slots))]
        slots = attend(1, block_mask, () if final else weights, slots)
        slots = dict(enumerate(slots))
        slots = exchange(slots)
        joined = finish(video, videos, [slots[index] for index in range(len(slots))], joined)
    return joined


def solution(mesh):
    placed = (
        P("stretch", None, "fsdp", None),
        P("stretch", None),
        P(),
        P(),
        P(None, "fsdp"),
        P(None, "fsdp"),
        P(None, "fsdp"),
    )

    def mapped(body):
        return jax.shard_map(
            body, mesh=mesh, in_specs=placed, out_specs=P("stretch", None, None, "fsdp"), check_vma=False
        )

    def run(*args):
        latents, w_query = args[0], args[4]
        parts = mesh.shape["stretch"], mesh.shape["fsdp"]
        share = latents.shape[2] // parts[1]
        heads = w_query.shape[1] // parts[1] // HEAD_DIM
        if parts[1] == 4 and heads == parts[0] == 8 and share % 16 == 0:
            return mapped(shards)(*args)
        return mapped(plain_shards)(*args)

    return run
```
